1024 devices in a mesh: seq: 32 (over x_hi, y), tensor: 8 (over z), fsdp: 4 (over x_lo, core).
Axes of the slice: x: 8 (x_hi: 4, x_lo: 2; x = x_hi * 2 + x_lo), y: 8, z: 8, core: 2. Of those that a mesh axis runs over, the one named last changes fastest.
Arguments:
- queries: bfloat16 [4, 8192, 2048], P('fsdp', 'seq', 'tensor'), may hold values from -57 to 57
- keys: bfloat16 [4, 8192, 1024], P('fsdp', 'seq', 'tensor'), may hold values from -6 to 6
- values: bfloat16 [4, 8192, 1024], P('fsdp', 'seq', 'tensor'), may hold values from -6 to 6
- cotangent: bfloat16 [4, 8192, 5376], P('fsdp', 'seq', 'tensor'), may hold values from -96 to 96
- out_weight: bfloat16 [2048, 5376], P('tensor', 'fsdp'), may hold values from -0.078125 to 0.078125
Outputs:
- query_grads: bfloat16 [4, 8192, 2048], P('fsdp', 'seq', 'tensor')
- key_grads: bfloat16 [4, 8192, 1024], P('fsdp', 'seq', 'tensor')
- value_grads: bfloat16 [4, 8192, 1024], P('fsdp', 'seq', 'tensor')
The draws below stay inside these ranges and needn't reach their ends.
All inputs are finite; a program needn't handle non-finite values.
Results may differ from the reference program's by a relative error of at most 0.015.
Values may be sent and summed in bfloat16 or wider, within the bound.
No kernel may reach another device: no remote copies, remote signals or barrier semaphores. Data moves between devices by JAX's collectives and lax.ppermute only.
A program may use at most 32 MiB of HBM per device.

```python
import jax
import jax.numpy as jnp
from jax import lax

D = 5376
QUERY_HEADS = 16
KEY_VALUE_HEADS = 8
HEAD_SIZE = 128
WINDOW = 1024
TOK_DEV = 256
BATCH_SEQUENCES = 4
SEQUENCE_LENGTH = 8192
N_SEQ = 32


def joint_rows(key):
    query_key = jax.random.fold_in(key, 101)
    random_key_for_keys = jax.random.fold_in(key, 202)
    queries = jax.random.truncated_normal(query_key, -6.0, 6.0, (BATCH_SEQUENCES, SEQUENCE_LENGTH, QUERY_HEADS, HEAD_SIZE), jnp.float32)
    key_row_block = jax.random.truncated_normal(random_key_for_keys, -6.0, 6.0, (BATCH_SEQUENCES, SEQUENCE_LENGTH, KEY_VALUE_HEADS, HEAD_SIZE), jnp.float32)
    return (queries.reshape(BATCH_SEQUENCES, SEQUENCE_LENGTH, QUERY_HEADS * HEAD_SIZE), key_row_block.reshape(BATCH_SEQUENCES, SEQUENCE_LENGTH, KEY_VALUE_HEADS * HEAD_SIZE))


def draw_queries(key, part):
    return joint_rows(key)[0].astype(jnp.bfloat16)


def draw_keys(key, part):
    return joint_rows(key)[1].astype(jnp.bfloat16)


def steps_of(rng, shape, cuts, least, high):
    gain, own = 1.0, jax.random.fold_in(rng, 6)
    for dim, parts in cuts:
        heights = jnp.exp(jax.random.uniform(jax.random.fold_in(own, dim), (parts,), jnp.float32, least / len(cuts), high / len(cuts)))
        gain = gain * jnp.repeat(heights, shape[dim] // parts).reshape([-1 if axis == dim else 1 for axis in range(len(shape))])
    return gain


def bell_draw(rng, shape, width, bound, shards=(), kind=jnp.bfloat16):
    gain = steps_of(rng, shape, shards, -0.22, 0.18) if shards else 1.0
    entries = jax.random.normal(rng, shape, jnp.float32) * width * gain
    return jnp.minimum(jnp.maximum(entries, -bound), bound).astype(kind)


def setup_inputs(seed: int = 0) -> dict:
    seeds = jax.random.split(jax.random.key(seed), 6)
    return {
        "queries": draw_queries(jax.random.fold_in(seeds[5], 71), 0),
        "keys": draw_keys(jax.random.fold_in(seeds[5], 71), 0),
        "values": bell_draw(seeds[2], (BATCH_SEQUENCES, SEQUENCE_LENGTH, KEY_VALUE_HEADS * HEAD_SIZE), 1.0, 6.0, ((0, 4), (1, 32), (2, 8))),
        "cotangent": bell_draw(seeds[3], (BATCH_SEQUENCES, SEQUENCE_LENGTH, D), 16.0, 96.0, ((0, 4), (1, 32), (2, 8))),
        "out_weight": bell_draw(seeds[4], (QUERY_HEADS * HEAD_SIZE, D), D ** -0.5, 0.078125, ((0, 8), (1, 4))),
    }


score_scale = 168.0 ** -0.5
masked_score = -1.0e30


def window_grads(query_rows, grad_rows, key_rows, value_rows, query_places, key_places):
    rows_here = query_rows.shape[0]
    key_span = key_rows.shape[0]
    kv_heads = key_rows.shape[1] // HEAD_SIZE
    head_groups = query_rows.shape[1] // (kv_heads * HEAD_SIZE)
    q_heads = query_rows.astype(jnp.float32).reshape(rows_here, kv_heads, head_groups, HEAD_SIZE)
    g_heads = grad_rows.astype(jnp.float32).reshape(rows_here, kv_heads, head_groups, HEAD_SIZE)
    k_heads = key_rows.astype(jnp.float32).reshape(key_span, kv_heads, HEAD_SIZE)
    v_heads = value_rows.astype(jnp.float32).reshape(key_span, kv_heads, HEAD_SIZE)
    scores = jnp.einsum("tkgd,skd->kgts", q_heads, k_heads) * score_scale
    allowed = (key_places[None, :] <= query_places[:, None]) & (key_places[None, :] > query_places[:, None] - WINDOW) & (key_places[None, :] >= 0)
    scores = jnp.where(allowed, scores, masked_score)
    top_score = jnp.max(scores, axis=-1, keepdims=True)
    log_totals = top_score + jnp.log(jnp.sum(jnp.exp(scores - top_score), axis=-1, keepdims=True))
    probs = jnp.exp(scores - log_totals)
    probs_low = lax.optimization_barrier(probs.astype(jnp.bfloat16)).astype(jnp.float32)
    attended = jnp.einsum("kgts,skd->tkgd", probs_low, v_heads)
    row_terms = jnp.transpose(jnp.sum(g_heads * attended, axis=-1), (1, 2, 0))
    grad_probs = jnp.einsum("tkgd,skd->kgts", g_heads, v_heads)
    grad_scores = probs * (grad_probs - row_terms[..., None])
    grad_low = lax.optimization_barrier(grad_scores.astype(jnp.bfloat16)).astype(jnp.float32)
    part_q = jnp.einsum("kgts,skd->tkgd", grad_low, k_heads) * score_scale
    part_k = jnp.einsum("kgts,tkgd->skd", grad_low, q_heads) * score_scale
    part_v = jnp.einsum("kgts,tkgd->skd", probs_low, g_heads)
    return part_q.reshape(rows_here, -1), part_k.reshape(key_span, -1), part_v.reshape(key_span, -1)


def reference(queries, keys, values, cotangent, out_weight):
    width_q = queries.shape[2]
    width_kv = keys.shape[2]
    key_span = WINDOW + TOK_DEV
    grads_q = []
    grads_k = []
    grads_v = []
    for batch_row in range(BATCH_SEQUENCES):
        head_grads = jnp.dot(cotangent[batch_row], out_weight.T, preferred_element_type=jnp.float32).astype(jnp.bfloat16)
        key_pad = jnp.concatenate([jnp.zeros((WINDOW, width_kv), keys.dtype), keys[batch_row]], axis=0)
        value_pad = jnp.concatenate([jnp.zeros((WINDOW, width_kv), values.dtype), values[batch_row]], axis=0)
        query_all = queries[batch_row]

        def block_step(totals, block_index):
            key_acc, value_acc = totals
            first_row = (block_index * TOK_DEV).astype(jnp.int32)
            query_rows = lax.dynamic_slice_in_dim(query_all, first_row, TOK_DEV, 0)
            grad_rows = lax.dynamic_slice_in_dim(head_grads, first_row, TOK_DEV, 0)
            key_rows = lax.dynamic_slice_in_dim(key_pad, first_row, key_span, 0)
            value_rows = lax.dynamic_slice_in_dim(value_pad, first_row, key_span, 0)
            query_places = first_row + jnp.arange(TOK_DEV, dtype=jnp.int32)
            key_places = first_row - WINDOW + jnp.arange(key_span, dtype=jnp.int32)
            part_q, part_k, part_v = window_grads(query_rows, grad_rows, key_rows, value_rows, query_places, key_places)
            key_acc = lax.dynamic_update_slice_in_dim(key_acc, lax.dynamic_slice_in_dim(key_acc, first_row, key_span, 0) + part_k, first_row, 0)
            value_acc = lax.dynamic_update_slice_in_dim(value_acc, lax.dynamic_slice_in_dim(value_acc, first_row, key_span, 0) + part_v, first_row, 0)
            return (key_acc, value_acc), part_q

        zero_acc = (jnp.zeros((WINDOW + SEQUENCE_LENGTH, width_kv), jnp.float32), jnp.zeros((WINDOW + SEQUENCE_LENGTH, width_kv), jnp.float32))
        final_acc, blocks_q = lax.scan(block_step, zero_acc, jnp.arange(N_SEQ, dtype=jnp.int32))
        grads_q.append(blocks_q.reshape(SEQUENCE_LENGTH, width_q).astype(jnp.bfloat16))
        grads_k.append(final_acc[0][WINDOW:].astype(jnp.bfloat16))
        grads_v.append(final_acc[1][WINDOW:].astype(jnp.bfloat16))
    return (jnp.stack(grads_q), jnp.stack(grads_k), jnp.stack(grads_v))
```

```python
import jax
import jax.numpy as jnp
from jax import lax
from jax.sharding import PartitionSpec as P

HEAD_SIZE = 128
WINDOW = 1024

score_scale = 168.0 ** (-0.5)
masked_score = -1e30


def along_seq(value, steps):
    count = lax.axis_size("seq")
    first, last = (max(0, -steps), min(count, count - steps))
    return lax.ppermute(value, "seq", [(source, source + steps) for source in range(first, last)])


def around_tensor(value, steps):
    count = lax.axis_size("tensor")
    return lax.ppermute(value, "tensor", [(i, (i + steps) % count) for i in range(count)])


def across_fsdp(value, mask):
    count = lax.axis_size("fsdp")
    return lax.ppermute(value, "fsdp", [(i, i ^ mask) for i in range(count)])


def window_probs(query_rows, key_rows, value_rows, query_places, key_places):
    scores = (
        jnp.einsum("tgd,sd->gts", query_rows, key_rows, preferred_element_type=jnp.float32)
        * score_scale
    )
    allowed = (
        (key_places[None, :] <= query_places[:, None])
        & (key_places[None, :] > query_places[:, None] - WINDOW)
        & (key_places[None, :] >= 0)
    )
    scores = jnp.where(allowed, scores, masked_score)
    top_score = jnp.max(scores, axis=-1, keepdims=True)
    log_totals = top_score + jnp.log(jnp.sum(jnp.exp(scores - top_score), axis=-1, keepdims=True))
    probs = jnp.exp(scores - log_totals)
    probs_low = probs.astype(jnp.bfloat16)
    attended = jnp.einsum("gts,sd->tgd", probs_low, value_rows, preferred_element_type=jnp.float32)
    return probs, probs_low, attended


def per_device(queries, keys, values, cotangent, out_weight):
    rows = queries.shape[1]
    seq_place = lax.axis_index("seq")
    tensor_place = lax.axis_index("tensor")
    fsdp_place = lax.axis_index("fsdp")
    reach = WINDOW // rows

    own_block = cotangent[0]
    blocks = {0: own_block}
    for steps in (1, -1, 2, -2):
        blocks[-steps] = around_tensor(own_block, steps)
    blocks[-3] = around_tensor(blocks[-2], 1)
    blocks[3] = around_tensor(blocks[2], -1)
    blocks[4] = around_tensor(blocks[2], -2)

    key_value = jnp.concatenate([keys[0], values[0]], axis=1)
    earlier = [along_seq(key_value, distance) for distance in range(reach, 0, -1)]

    width = cotangent.shape[2]
    weight_halves = jnp.stack([out_weight[:, :width], out_weight[:, width:]])
    weight_shards = [weight_halves] + [across_fsdp(weight_halves, mask) for mask in (1, 2, 3)]
    weight_blocks = jnp.concatenate(weight_shards, axis=0)

    window = jnp.concatenate(earlier + [key_value], axis=0)
    window_keys = window[:, :HEAD_SIZE]
    window_values = window[:, HEAD_SIZE:]
    query_heads = queries[0].reshape(rows, -1, HEAD_SIZE)
    first_place = seq_place * rows
    query_places = first_place + jnp.arange(rows, dtype=jnp.int32)
    key_places = first_place - WINDOW + jnp.arange(WINDOW + rows, dtype=jnp.int32)
    probs, probs_low, attended = window_probs(
        query_heads, window_keys, window_values, query_places, key_places
    )

    head_sums = 0.0
    for offset in (0, -1, 1, -2, 2, -3, 3, 4):
        block_at = lax.rem(tensor_place + offset + 8, 8)
        weight_at = (fsdp_place ^ (block_at // 2)) * 2 + lax.rem(block_at, 2)
        weight = lax.dynamic_index_in_dim(weight_blocks, weight_at, 0, keepdims=False)
        head_sums = head_sums + lax.dot_general(
            blocks[offset], weight, (((1,), (1,)), ((), ())), preferred_element_type=jnp.float32
        )
    grad_heads = head_sums.astype(jnp.bfloat16).reshape(rows, -1, HEAD_SIZE)

    row_terms = jnp.transpose(jnp.sum(grad_heads.astype(jnp.float32) * attended, axis=-1), (1, 0))
    grad_probs = jnp.einsum(
        "tgd,sd->gts", grad_heads, window_values, preferred_element_type=jnp.float32
    )
    grad_low = (probs * (grad_probs - row_terms[..., None])).astype(jnp.bfloat16)
    part_q = (
        jnp.einsum("gts,sd->tgd", grad_low, window_keys, preferred_element_type=jnp.float32)
        * score_scale
    )
    part_k = (
        jnp.einsum("gts,tgd->sd", grad_low, query_heads, preferred_element_type=jnp.float32)
        * score_scale
    )
    part_v = jnp.einsum("gts,tgd->sd", probs_low, grad_heads, preferred_element_type=jnp.float32)
    part = jnp.concatenate([part_k, part_v], axis=1).reshape(reach + 1, rows, -1)

    total = part[reach]
    for distance in range(reach, 0, -1):
        returned = along_seq(part[reach - distance].astype(jnp.bfloat16), -distance)
        total = total + returned.astype(jnp.float32)
    total = total.astype(jnp.bfloat16)
    return (
        part_q.reshape(1, rows, -1).astype(jnp.bfloat16),
        total[None, :, :HEAD_SIZE],
        total[None, :, HEAD_SIZE:],
    )


def solution(mesh):
    return jax.shard_map(
        per_device,
        mesh=mesh,
        in_specs=(
            P("fsdp", "seq", "tensor"),
            P("fsdp", "seq", "tensor"),
            P("fsdp", "seq", "tensor"),
            P("fsdp", "seq", "tensor"),
            P("tensor", "fsdp"),
        ),
        out_specs=(
            P("fsdp", "seq", "tensor"),
            P("fsdp", "seq", "tensor"),
            P("fsdp", "seq", "tensor"),
        ),
        check_vma=False,
    )
```
